32 devices in a mesh: dp: 16 (over z, x, core), tensor: 2 (over y).
Axes of the slice: x: 2, y: 2, z: 4, core: 2. Of those that a mesh axis runs over, the one named last changes fastest.
Arguments:
- block_input: float32 [20480, 1024], P(('dp', 'tensor')), may hold values from -6 to 6
- input_gain: bfloat16 [1024], P(('dp', 'tensor')), may hold values from 0.5 to 1.5
- proj_gate: bfloat16 [1024, 2048], P('dp', 'tensor'), may hold values from -0.1875 to 0.1875
- proj_inner: bfloat16 [1024, 2048], P('dp', 'tensor'), may hold values from -0.1875 to 0.1875
- proj_step: bfloat16 [1024, 32], P('dp', 'tensor'), may hold values from -0.1875 to 0.1875
- proj_output: bfloat16 [1024, 2048], P('dp', 'tensor'), may hold values from -0.125 to 0.125
- proj_state: bfloat16 [1024, 256], P(('dp', 'tensor')), may hold values from -0.1875 to 0.1875
- conv_inner: float32 [4, 2048], P(None, 'tensor'), may hold values from -3 to 3
- conv_inner_bias: float32 [2048], P('tensor'), may hold values from -3 to 3
- conv_state: float32 [4, 256], replicated, may hold values from -3 to 3
- conv_state_bias: float32 [256], replicated, may hold values from -3 to 3
- decay_log: float32 [32], P('tensor'), may hold values from -1 to 2.5
- step_bias: float32 [32], P('tensor'), may hold values from -6 to -2
- skip_gain: float32 [32], P('tensor'), may hold values from 0.5 to 1.5
- gate_gain: float32 [2048], P('tensor'), may hold values from 0.5 to 1.5
- cotangent: float32 [20480, 1024], P(('dp', 'tensor')), may hold values from -6 to 6
Outputs:
- block_output: float32 [20480, 1024], P(('dp', 'tensor'))
- grad_input: float32 [20480, 1024], P(('dp', 'tensor'))
- grad_input_gain: float32 [1024], P(('dp', 'tensor'))
- grad_proj_gate: float32 [1024, 2048], P('dp', 'tensor')
- grad_proj_inner: float32 [1024, 2048], P('dp', 'tensor')
- grad_proj_step: float32 [1024, 32], P('dp', 'tensor')
- grad_proj_output: float32 [1024, 2048], P('dp', 'tensor')
- grad_proj_state: float32 [1024, 256], P(('dp', 'tensor'))
- grad_conv_inner: float32 [4, 2048], P(None, 'tensor')
- grad_conv_inner_bias: float32 [2048], P('tensor')
- grad_conv_state: float32 [4, 256], replicated
- grad_conv_state_bias: float32 [256], replicated
- grad_decay_log: float32 [32], P('tensor')
- grad_step_bias: float32 [32], P('tensor')
- grad_skip_gain: float32 [32], P('tensor')
- grad_gate_gain: float32 [2048], P('tensor')
The draws below stay inside these ranges and needn't reach their ends.
All inputs are finite; a program needn't handle non-finite values.
Results may differ from the reference program's by a relative error of at most 0.011.
Values may be sent and summed in bfloat16 or wider, within the bound.
A program may use at most 256 MiB of HBM per device.

```python
import jax
import jax.numpy as jnp
from jax import lax

D = 1024
HEADS = 32
STATE = 128
KW = 4
BLOCK = 256
LEN = 1280
INNER = 2048
TOKENS = 20480


def level_of(rng, shape, split, smallest, largest):
    gain = 1.0
    for dim, shards_of in split:
        steps = jax.random.uniform(jax.random.fold_in(jax.random.fold_in(rng, 6), dim), (shards_of,), jnp.float32, smallest / len(split), largest / len(split))
        gain = gain * jnp.repeat(jnp.exp(steps), shape[dim] // shards_of).reshape((-1,) + (1,) * (len(shape) - 1 - dim))
    return gain


def bell_draw(key, dims, deviation, reach, split=(), dtype=jnp.bfloat16):
    values = jax.random.normal(key, dims, jnp.float32) * deviation
    if len(split) > 0:
        values = level_of(key, dims, split, -0.22, 0.18) * values
    return jnp.clip(values, min=-reach, max=reach).astype(dtype)


def setup_inputs(seed: int = 0) -> dict:
    key_of = jax.random.split(jax.random.key(seed), 17)
    block_input = bell_draw(key_of[0], (TOKENS, D), 1.0, 6.0, ((0, 32),), jnp.float32)
    input_gain = jnp.clip(1.0 + 0.1 * jax.random.normal(key_of[1], (D,), jnp.float32), 0.5, 1.5).astype(jnp.bfloat16)
    proj_gate = bell_draw(key_of[2], (D, INNER), D ** -0.5, 0.1875, ((0, 16), (1, 2)))
    proj_inner = bell_draw(key_of[3], (D, INNER), D ** -0.5, 0.1875, ((0, 16), (1, 2)))
    proj_step = bell_draw(key_of[4], (D, HEADS), D ** -0.5, 0.1875, ((0, 16), (1, 2)))
    proj_output = bell_draw(key_of[5], (D, INNER), INNER ** -0.5, 0.125, ((0, 16), (1, 2)))
    proj_state = bell_draw(key_of[6], (D, 2 * STATE), D ** -0.5, 0.1875, ((0, 32),))
    conv_inner = bell_draw(key_of[7], (KW, INNER), KW ** -0.5, 3.0, ((1, 2),), jnp.float32)
    conv_inner_bias = bell_draw(key_of[8], (INNER,), 0.5, 3.0, ((0, 2),), jnp.float32)
    conv_state = bell_draw(key_of[9], (KW, 2 * STATE), KW ** -0.5, 3.0, (), jnp.float32)
    conv_state_bias = bell_draw(key_of[10], (2 * STATE,), 0.5, 3.0, (), jnp.float32)
    decay_log = jnp.clip(-1.0 + 3.5 * jax.random.uniform(key_of[11], (HEADS,), jnp.float32) ** level_of(key_of[11], (HEADS,), ((0, 2),), -0.2, 0.2), -1.0, 2.5)
    step_bias = jnp.clip(-6.0 + 4.0 * jax.random.uniform(key_of[12], (HEADS,), jnp.float32) ** level_of(key_of[12], (HEADS,), ((0, 2),), -0.2, 0.2), -6.0, -2.0)
    skip_gain = jnp.clip(0.5 + 1.0 * jax.random.uniform(key_of[13], (HEADS,), jnp.float32) ** level_of(key_of[13], (HEADS,), ((0, 2),), -0.2, 0.2), 0.5, 1.5)
    gate_gain = jnp.clip(1.0 + 0.1 * jax.random.normal(key_of[14], (INNER,), jnp.float32), 0.5, 1.5)
    cotangent = bell_draw(key_of[15], (TOKENS, D), 1.0, 6.0, ((0, 32),), jnp.float32)
    return {"block_input": block_input, "input_gain": input_gain, "proj_gate": proj_gate, "proj_inner": proj_inner, "proj_step": proj_step, "proj_output": proj_output, "proj_state": proj_state, "conv_inner": conv_inner, "conv_inner_bias": conv_inner_bias, "conv_state": conv_state, "conv_state_bias": conv_state_bias, "decay_log": decay_log, "step_bias": step_bias, "skip_gain": skip_gain, "gate_gain": gate_gain, "cotangent": cotangent}


epsilon = 1e-05

def causal_conv(signal, kernel, offset):
    width = kernel.shape[0]
    length = signal.shape[1]
    padded = jnp.pad(signal, ((0, 0), (width - 1, 0), (0, 0)))
    result = offset + jnp.zeros_like(signal)
    for tap in range(width):
        result = result + kernel[tap] * padded[:, tap:tap + length]
    return result

def scan_heads(inner_in, entry_in, read_in, step_size, decay_rate, skip_weight):
    seq_count, length, heads, width = inner_in.shape
    blocks = length // BLOCK
    highest = lax.Precision.HIGHEST
    inner_blk = inner_in.reshape(seq_count, blocks, BLOCK, heads, width)
    entry_blk = entry_in.reshape(seq_count, blocks, BLOCK, entry_in.shape[-1])
    read_blk = read_in.reshape(seq_count, blocks, BLOCK, read_in.shape[-1])
    step_blk = step_size.reshape(seq_count, blocks, BLOCK, heads)
    running = jnp.cumsum(step_blk * decay_rate, axis=2)
    lower = (jnp.arange(BLOCK)[:, None] >= jnp.arange(BLOCK)[None, :])[None, None, :, :, None]
    spread = running[:, :, :, None, :] - running[:, :, None, :, :]
    mixing = jnp.where(lower, jnp.exp(jnp.where(lower, spread, 0.0)), 0.0)
    intersection = jnp.einsum('scin,scjn->scij', read_blk, entry_blk, precision=highest)
    weights = mixing * intersection[..., None] * step_blk[:, :, None, :, :]
    local_part = jnp.einsum('scijh,scjhp->scihp', weights, inner_blk, precision=highest)
    to_end = jnp.exp(running[:, :, -1:, :] - running) * step_blk
    block_states = jnp.einsum('scjn,scjh,scjhp->schpn', entry_blk, to_end, inner_blk, precision=highest)
    totals = jnp.exp(running[:, :, -1, :])

    def carry_step(carry, pieces):
        total, fresh = pieces
        return (total[:, :, None, None] * carry + fresh, carry)
    start = jnp.zeros((seq_count, heads, width, entry_blk.shape[-1]), jnp.float32)
    final_state, entering = lax.scan(carry_step, start, (jnp.moveaxis(totals, 1, 0), jnp.moveaxis(block_states, 1, 0)))
    entering = jnp.moveaxis(entering, 0, 1)
    carried = jnp.einsum('scin,schpn->scihp', read_blk, entering, precision=highest) * jnp.exp(running)[..., None]
    result = local_part + carried + skip_weight[:, None] * inner_blk
    return result.reshape(seq_count, length, heads, width)

def mixer_core(inner_raw, state_raw, step_raw, gate_raw, conv_inner, conv_inner_bias, conv_state, conv_state_bias, decay_log, step_bias, skip_gain):
    heads = step_raw.shape[-1]
    inner_act = jax.nn.silu(causal_conv(inner_raw, conv_inner, conv_inner_bias))
    state_act = jax.nn.silu(causal_conv(state_raw, conv_state, conv_state_bias))
    step_size = jax.nn.softplus(step_raw + step_bias)
    decay_rate = -jnp.exp(decay_log)
    seq_count, length, channels = inner_act.shape
    scanned = scan_heads(inner_act.reshape(seq_count, length, heads, channels // heads), state_act[..., :STATE], state_act[..., STATE:], step_size, decay_rate, skip_gain)
    return scanned.reshape(seq_count, length, channels) * jax.nn.silu(gate_raw)

def reference(block_input, input_gain, proj_gate, proj_inner, proj_step, proj_output, proj_state, conv_inner, conv_inner_bias, conv_state, conv_state_bias, decay_log, step_bias, skip_gain, gate_gain, cotangent):
    seq_total = block_input.shape[0] // LEN
    sources = block_input.reshape(seq_total, LEN, D)
    upstreams = cotangent.reshape(seq_total, LEN, D)
    gain_wide = input_gain.astype(jnp.float32)

    def one_sequence(totals, pieces):
        source, upstream = pieces
        inv_in = lax.rsqrt(lax.optimization_barrier(jnp.mean(source * source, axis=-1, keepdims=True)) + epsilon)
        normed = (source * inv_in * gain_wide).astype(jnp.bfloat16)
        gate_raw = jnp.dot(normed, proj_gate, preferred_element_type=jnp.float32)
        inner_raw = jnp.dot(normed, proj_inner, preferred_element_type=jnp.float32)
        step_raw = jnp.dot(normed, proj_step, preferred_element_type=jnp.float32)
        state_raw = jnp.dot(normed, proj_state, preferred_element_type=jnp.float32)
        gated, core_back = jax.vjp(mixer_core, inner_raw[None], state_raw[None], step_raw[None], gate_raw[None], conv_inner, conv_inner_bias, conv_state, conv_state_bias, decay_log, step_bias, skip_gain)
        gated = gated[0]
        inv_gate = lax.rsqrt(lax.optimization_barrier(jnp.mean(gated * gated, axis=-1, keepdims=True)) + epsilon)
        normed_gate = (gated * inv_gate * gate_gain).astype(jnp.bfloat16)
        block_output = source + jnp.dot(normed_gate, proj_output.T, preferred_element_type=jnp.float32)
        cot = upstream.astype(jnp.bfloat16)
        grad_output_w = jnp.dot(cot.T, normed_gate, preferred_element_type=jnp.float32)
        grad_normed = jnp.dot(cot, proj_output, preferred_element_type=jnp.float32)
        grad_gain_gate = lax.optimization_barrier(jnp.sum(grad_normed * gated * inv_gate, axis=0))
        scaled = grad_normed * gate_gain
        grad_gated = inv_gate * (scaled - gated * inv_gate * inv_gate * lax.optimization_barrier(jnp.mean(scaled * gated, axis=-1, keepdims=True)))
        core_grads = core_back(grad_gated[None])
        inner_back = core_grads[0][0].astype(jnp.bfloat16)
        state_back = core_grads[1][0].astype(jnp.bfloat16)
        step_back = core_grads[2][0].astype(jnp.bfloat16)
        gate_back = core_grads[3][0].astype(jnp.bfloat16)
        grad_gate_w = jnp.dot(normed.T, gate_back, preferred_element_type=jnp.float32)
        grad_inner_w = jnp.dot(normed.T, inner_back, preferred_element_type=jnp.float32)
        grad_step_w = jnp.dot(normed.T, step_back, preferred_element_type=jnp.float32)
        grad_state_w = jnp.dot(normed.T, state_back, preferred_element_type=jnp.float32)
        grad_normed_in = jnp.dot(gate_back, proj_gate.T, preferred_element_type=jnp.float32)
        grad_normed_in = grad_normed_in + jnp.dot(inner_back, proj_inner.T, preferred_element_type=jnp.float32)
        grad_normed_in = grad_normed_in + jnp.dot(step_back, proj_step.T, preferred_element_type=jnp.float32)
        grad_normed_in = grad_normed_in + jnp.dot(state_back, proj_state.T, preferred_element_type=jnp.float32)
        grad_gain_in = lax.optimization_barrier(jnp.sum(grad_normed_in * source * inv_in, axis=0))
        scaled_in = grad_normed_in * gain_wide
        grad_source = upstream + inv_in * (scaled_in - source * inv_in * inv_in * lax.optimization_barrier(jnp.mean(scaled_in * source, axis=-1, keepdims=True)))
        fresh = (grad_gain_in, grad_gate_w, grad_inner_w, grad_step_w, grad_output_w, grad_state_w, core_grads[4], core_grads[5], core_grads[6], core_grads[7], core_grads[8], core_grads[9], core_grads[10], grad_gain_gate)
        totals = jax.tree.map(lambda left, right: left + right, totals, fresh)
        return (totals, (block_output, grad_source))
    shapes = (input_gain.shape, proj_gate.shape, proj_inner.shape, proj_step.shape, proj_output.shape, proj_state.shape, conv_inner.shape, conv_inner_bias.shape, conv_state.shape, conv_state_bias.shape, decay_log.shape, step_bias.shape, skip_gain.shape, gate_gain.shape)
    start = tuple((jnp.zeros(shape, jnp.float32) for shape in shapes))
    totals, stacked = lax.scan(one_sequence, start, (sources, upstreams))
    block_output = stacked[0].reshape(block_input.shape[0], D)
    grad_input = stacked[1].reshape(block_input.shape[0], D)
    return (block_output, grad_input, totals[0], totals[1], totals[2], totals[3], totals[4], totals[5], totals[6], totals[7], totals[8], totals[9], totals[10], totals[11], totals[12], totals[13])
```

```python
import jax
import jax.numpy as jnp
from jax import lax
from jax.sharding import PartitionSpec as P

HEADS = 32
STATE = 128
BLOCK = 256
LEN = 1280
INNER = 2048


epsilon = 1e-05


def swap(values, axis, bit):
    size = lax.axis_size(axis)
    return lax.ppermute(values, axis, [(i, i ^ (1 << bit)) for i in range(size)])


def bits_of(axis):
    size = lax.axis_size(axis)
    bits = size.bit_length() - 1
    return bits if (1 << bits) == size else None


def gather_rows(values, axis):
    bits = bits_of(axis)
    if bits is None:
        return lax.all_gather(values, axis, axis=0, tiled=True)
    index = lax.axis_index(axis)
    rows, width = values.shape
    whole = values[None]
    for bit in reversed(range(bits)):
        other = swap(whole, axis, bit)
        high = ((index >> bit) & 1) == 1
        low_part = jnp.where(high, other, whole)
        high_part = jnp.where(high, whole, other)
        whole = jnp.stack([low_part, high_part], axis=1).reshape(-1, rows, width)
    return whole.reshape(-1, width)


def scatter_rows(values, axis):
    bits = bits_of(axis)
    if bits is None:
        return lax.psum_scatter(values, axis, scatter_dimension=0, tiled=True)
    index = lax.axis_index(axis)
    size = 1 << bits
    width = values.shape[-1]
    part = values.reshape(size, values.shape[0] // size, width)
    rows = part.shape[1]
    for bit in range(bits):
        pairs = part.reshape(-1, 2, rows, width)
        mine = (index >> bit) & 1
        keep = lax.dynamic_index_in_dim(pairs, mine, 1, keepdims=False)
        send = lax.dynamic_index_in_dim(pairs, 1 - mine, 1, keepdims=False)
        part = keep + swap(send.astype(jnp.bfloat16), axis, bit).astype(jnp.float32)
    return part.reshape(rows, width)


def sum_all(values, axis):
    bits = bits_of(axis)
    if bits is None:
        return lax.psum(values, axis)
    for bit in range(bits):
        values = values + swap(values, axis, bit)
    return values


def causal_conv(signal, kernel, offset):
    width = kernel.shape[0]
    length = signal.shape[1]
    padded = jnp.pad(signal, ((0, 0), (width - 1, 0), (0, 0)))
    result = offset + jnp.zeros_like(signal)
    for tap in range(width):
        result = result + kernel[tap] * padded[:, tap : tap + length]
    return result


def scan_heads(inner_in, entry_in, read_in, step_size, decay_rate, skip_weight):
    seq_count, length, heads, width = inner_in.shape
    blocks = length // BLOCK
    highest = lax.Precision.DEFAULT
    inner_blk = jnp.swapaxes(
        inner_in.reshape(seq_count, blocks, BLOCK, heads * width), 2, 3
    ).reshape(seq_count, blocks, heads, width, BLOCK)
    entry_blk = entry_in.reshape(seq_count, blocks, BLOCK, entry_in.shape[-1])
    read_blk = read_in.reshape(seq_count, blocks, BLOCK, read_in.shape[-1])
    step_major = jnp.swapaxes(step_size.reshape(seq_count, blocks, BLOCK, heads), 2, 3)
    lower = jnp.arange(BLOCK)[:, None] >= jnp.arange(BLOCK)[None, :]
    running = jnp.einsum(
        "schj,ij->schi",
        step_major * decay_rate[:, None],
        lower.astype(jnp.float32),
        precision=lax.Precision.HIGHEST,
    )
    lower = lower[None, None, None, :, :]
    spread = running[:, :, :, :, None] - running[:, :, :, None, :]
    mixing = jnp.where(lower, jnp.exp(jnp.where(lower, spread, 0.0)), 0.0)
    intersection = jnp.einsum("scin,scjn->scij", read_blk, entry_blk, precision=highest)
    stepped = inner_blk * step_major[:, :, :, None, :]
    weights = mixing * intersection[:, :, None, :, :]
    local_part = jnp.einsum("schpj,schij->schpi", stepped, weights, precision=highest)
    to_end = jnp.exp(running[:, :, :, -1:] - running)
    block_states = jnp.einsum(
        "schpj,scjn->schpn", stepped * to_end[:, :, :, None, :], entry_blk, precision=highest
    )
    totals = jnp.exp(running[:, :, :, -1])
    carry = jnp.zeros((seq_count, heads, width, entry_blk.shape[-1]), jnp.float32)
    entering = []
    for block in range(blocks):
        entering.append(carry)
        carry = totals[:, block, :, None, None] * carry + block_states[:, block]
    entering = jnp.stack(entering, axis=1)
    carried = (
        jnp.einsum("schpn,scin->schpi", entering, read_blk, precision=highest)
        * jnp.exp(running)[:, :, :, None, :]
    )
    result = local_part + carried + skip_weight[:, None, None] * inner_blk
    result = jnp.swapaxes(result.reshape(seq_count, blocks, heads * width, BLOCK), 2, 3)
    return result.reshape(seq_count, length, heads, width)


def mixer_core(
    inner_raw,
    state_raw,
    step_raw,
    conv_inner,
    conv_inner_bias,
    conv_state,
    conv_state_bias,
    decay_log,
    step_bias,
    skip_gain,
):
    heads = step_raw.shape[-1]
    inner_act = jax.nn.silu(causal_conv(inner_raw, conv_inner, conv_inner_bias))
    state_act = jax.nn.silu(causal_conv(state_raw, conv_state, conv_state_bias))
    step_size = jax.nn.softplus(step_raw + step_bias)
    decay_rate = -jnp.exp(decay_log)
    seq_count, length, channels = inner_act.shape
    scanned = scan_heads(
        inner_act.reshape(seq_count, length, heads, channels // heads),
        state_act[..., :STATE],
        state_act[..., STATE:],
        step_size,
        decay_rate,
        skip_gain,
    )
    return scanned.reshape(seq_count, length, channels)


def on_device(
    block_input,
    input_gain,
    proj_gate,
    proj_inner,
    proj_step,
    proj_output,
    proj_state,
    conv_inner,
    conv_inner_bias,
    conv_state,
    conv_state_bias,
    decay_log,
    step_bias,
    skip_gain,
    gate_gain,
    cotangent,
):
    state_width = proj_state.shape[-1]
    state_gain = gather_rows(
        gather_rows(jnp.concatenate([proj_state, input_gain[:, None]], axis=1), "tensor"), "dp"
    )
    state_w = state_gain[:, :state_width]
    gain_rows = state_gain[:, state_width]
    gain_wide = gain_rows.astype(jnp.float32)
    inv_in = lax.rsqrt(jnp.mean(block_input * block_input, axis=-1, keepdims=True) + epsilon)
    normed_own = (block_input * inv_in * gain_wide).astype(jnp.bfloat16)
    normed = gather_rows(normed_own, "tensor")
    gate_w, inner_w, step_w, output_w = (
        lax.all_gather(proj_gate, "dp", axis=0, tiled=True),
        gather_rows(proj_inner, "dp"),
        gather_rows(proj_step, "dp"),
        lax.all_gather(proj_output, "dp", axis=0, tiled=True),
    )
    group_rows = normed.shape[0]
    seq_count = group_rows // LEN
    gate_raw = jnp.dot(normed, gate_w, preferred_element_type=jnp.float32)
    inner_raw = jnp.dot(normed, inner_w, preferred_element_type=jnp.float32)
    step_raw = jnp.dot(normed, step_w, preferred_element_type=jnp.float32)
    state_raw = jnp.dot(normed, state_w, preferred_element_type=jnp.float32)

    def shaped(values):
        return values.reshape(seq_count, LEN, values.shape[-1])

    scanned, core_back = jax.vjp(
        mixer_core,
        shaped(inner_raw),
        shaped(state_raw),
        shaped(step_raw),
        conv_inner,
        conv_inner_bias,
        conv_state,
        conv_state_bias,
        decay_log,
        step_bias,
        skip_gain,
    )
    gated, gate_rule = jax.vjp(
        lambda scan, gate: scan * jax.nn.silu(gate), scanned.reshape(group_rows, -1), gate_raw
    )
    squares = lax.psum(jnp.sum(gated * gated, axis=-1), "tensor")
    inv_gate = lax.rsqrt(squares[:, None] / INNER + epsilon)
    normed_gate = (gated * inv_gate * gate_gain).astype(jnp.bfloat16)
    branch_sum = scatter_rows(
        jnp.dot(normed_gate, output_w.T, preferred_element_type=jnp.float32), "tensor"
    )
    block_output = block_input + branch_sum
    cot_full = gather_rows(cotangent.astype(jnp.bfloat16), "tensor")
    grad_output_w = jnp.dot(cot_full.T, normed_gate, preferred_element_type=jnp.float32)
    grad_normed = jnp.dot(cot_full, output_w, preferred_element_type=jnp.float32)
    grad_gain_gate = jnp.sum(grad_normed * gated * inv_gate, axis=0)
    scaled = grad_normed * gate_gain
    products = lax.psum(jnp.sum(scaled * gated, axis=-1), "tensor")
    grad_gated = inv_gate * (scaled - gated * inv_gate * inv_gate * products[:, None] / INNER)
    grad_scanned, gate_back = gate_rule(grad_gated)
    gate_back = gate_back.astype(jnp.bfloat16)
    grad_gate_w = jnp.dot(normed.T, gate_back, preferred_element_type=jnp.float32)
    grad_scanned, grad_gate_w, grad_output_w = lax.optimization_barrier(
        (grad_scanned, grad_gate_w, grad_output_w)
    )
    core_grads = core_back(grad_scanned.reshape(seq_count, LEN, -1))
    inner_back = core_grads[0].reshape(group_rows, -1).astype(jnp.bfloat16)
    state_part = core_grads[1].reshape(group_rows, -1)
    step_back = core_grads[2].reshape(group_rows, -1).astype(jnp.bfloat16)
    grad_inner_w = jnp.dot(normed.T, inner_back, preferred_element_type=jnp.float32)
    grad_step_w = jnp.dot(normed.T, step_back, preferred_element_type=jnp.float32)
    partial_in = jnp.dot(gate_back, gate_w.T, preferred_element_type=jnp.float32)
    partial_in = partial_in + jnp.dot(inner_back, inner_w.T, preferred_element_type=jnp.float32)
    partial_in = partial_in + jnp.dot(step_back, step_w.T, preferred_element_type=jnp.float32)
    summed_in, state_sum = (
        scatter_rows(partial_in, "tensor"),
        scatter_rows(state_part, "tensor"),
    )
    state_back = state_sum.astype(jnp.bfloat16)
    grad_normed_in = summed_in + jnp.dot(state_back, state_w.T, preferred_element_type=jnp.float32)
    grad_gain_in = jnp.sum(grad_normed_in * block_input * inv_in, axis=0)
    scaled_in = grad_normed_in * gain_wide
    grad_input = cotangent + inv_in * (
        scaled_in
        - block_input * inv_in * inv_in * jnp.mean(scaled_in * block_input, axis=-1, keepdims=True)
    )
    grad_state_w = jnp.dot(normed_own.T, state_back, preferred_element_type=jnp.float32)
    grad_output_own = scatter_rows(grad_output_w, "dp")
    grad_gate_own = scatter_rows(grad_gate_w, "dp")
    grad_inner_own = scatter_rows(grad_inner_w, "dp")
    step_width = grad_step_w.shape[-1]
    narrow_own = scatter_rows(
        jnp.concatenate([grad_state_w, grad_gain_in[:, None], grad_step_w], axis=1), "dp"
    )
    grad_step_own = narrow_own[:, state_width + 1 :]
    state_own = scatter_rows(narrow_own[:, : state_width + 1], "tensor")
    grad_state_own = state_own[:, :state_width]
    grad_gain_own = state_own[:, state_width]
    smalls = list(core_grads[3:10]) + [grad_gain_gate]
    order = [0, 1, 4, 5, 6, 7, 2, 3]
    split = sum(smalls[k].size for k in order[:6])
    packed = sum_all(jnp.concatenate([smalls[k].reshape(-1) for k in order]), "dp")
    packed = jnp.concatenate([packed[:split], sum_all(packed[split:], "tensor")])
    summed_small = [None] * 8
    start = 0
    for k in order:
        summed_small[k] = packed[start : start + smalls[k].size].reshape(smalls[k].shape)
        start += smalls[k].size
    return (
        block_output,
        grad_input,
        grad_gain_own,
        grad_gate_own,
        grad_inner_own,
        grad_step_own,
        grad_output_own,
        grad_state_own,
        summed_small[0],
        summed_small[1],
        summed_small[2],
        summed_small[3],
        summed_small[4],
        summed_small[5],
        summed_small[6],
        summed_small[7],
    )


def solution(mesh):
    return jax.shard_map(
        on_device,
        mesh=mesh,
        in_specs=(
            P(("dp", "tensor"), None),
            P(("dp", "tensor")),
            P("dp", "tensor"),
            P("dp", "tensor"),
            P("dp", "tensor"),
            P("dp", "tensor"),
            P(("dp", "tensor"), None),
            P(None, "tensor"),
            P("tensor"),
            P(),
            P(),
            P("tensor"),
            P("tensor"),
            P("tensor"),
            P("tensor"),
            P(("dp", "tensor"), None),
        ),
        out_specs=(
            P(("dp", "tensor"), None),
            P(("dp", "tensor"), None),
            P(("dp", "tensor")),
            P("dp", "tensor"),
            P("dp", "tensor"),
            P("dp", "tensor"),
            P("dp", "tensor"),
            P(("dp", "tensor"), None),
            P(None, "tensor"),
            P("tensor"),
            P(),
            P(),
            P("tensor"),
            P("tensor"),
            P("tensor"),
            P("tensor"),
        ),
        check_vma=False,
    )
```
